32 devices in a mesh: fsdp: 8 (over z, x), tp: 4 (over y, core).
Axes of the slice: x: 2, y: 2, z: 4, core: 2. Of those that a mesh axis runs over, the one named last changes fastest.
Arguments:
- tokens_in: bfloat16 [8, 577, 1024], P('fsdp'), may hold values from -6 to 6
- cotangent: bfloat16 [8, 577, 1024], P('fsdp'), may hold values from -6 to 6
- w_query: float32 [2, 1024, 1024], P(None, 'fsdp', 'tp'), may hold values from -0.1875 to 0.1875
- w_key: float32 [2, 1024, 1024], P(None, 'fsdp', 'tp'), may hold values from -0.1875 to 0.1875
- w_value: float32 [2, 1024, 1024], P(None, 'fsdp', 'tp'), may hold values from -0.1875 to 0.1875
- w_out: float32 [2, 1024, 1024], P(None, 'tp', 'fsdp'), may hold values from -0.5 to 0.5
- w_fc1: float32 [2, 1024, 4096], P(None, 'fsdp', 'tp'), may hold values from -0.1875 to 0.1875
- w_fc2: float32 [2, 4096, 1024], P(None, 'tp', 'fsdp'), may hold values from -0.09375 to 0.09375
- mom_query: float32 [2, 1024, 1024], P(None, 'fsdp', 'tp'), may hold values from -48 to 48
- mom_key: float32 [2, 1024, 1024], P(None, 'fsdp', 'tp'), may hold values from -48 to 48
- mom_value: float32 [2, 1024, 1024], P(None, 'fsdp', 'tp'), may hold values from -256 to 256
- mom_out: float32 [2, 1024, 1024], P(None, 'tp', 'fsdp'), may hold values from -128 to 128
- mom_fc1: float32 [2, 1024, 4096], P(None, 'fsdp', 'tp'), may hold values from -128 to 128
- mom_fc2: float32 [2, 4096, 1024], P(None, 'tp', 'fsdp'), may hold values from -256 to 256
- vectors: float32 [2, 8, 1024], replicated, may hold values from -1 to 1.3, as said below
- fc1_bias: float32 [2, 4096], replicated, may hold values from -3 to 3
- vec_first: float32 [2, 8, 1024], replicated, may hold values from -32 to 32
- vec_second: float32 [2, 8, 1024], replicated, may hold values from 20 to 400
- bias_first: float32 [2, 4096], replicated, may hold values from -16 to 16
- bias_second: float32 [2, 4096], replicated, may hold values from 5 to 100
Outputs:
- tokens_out: bfloat16 [8, 577, 1024], P('fsdp')
- input_grad: float32 [8, 577, 1024], P('fsdp')
- grad_query: float32 [2, 1024, 1024], P(None, 'fsdp', 'tp')
- grad_key: float32 [2, 1024, 1024], P(None, 'fsdp', 'tp')
- grad_value: float32 [2, 1024, 1024], P(None, 'fsdp', 'tp')
- grad_out: float32 [2, 1024, 1024], P(None, 'tp', 'fsdp')
- grad_fc1: float32 [2, 1024, 4096], P(None, 'fsdp', 'tp')
- grad_fc2: float32 [2, 4096, 1024], P(None, 'tp', 'fsdp')
- grad_vectors: float32 [2, 8, 1024], replicated
- grad_fc1_bias: float32 [2, 4096], replicated
- new_query: float32 [2, 1024, 1024], P(None, 'fsdp', 'tp')
- new_key: float32 [2, 1024, 1024], P(None, 'fsdp', 'tp')
- new_value: float32 [2, 1024, 1024], P(None, 'fsdp', 'tp')
- new_out: float32 [2, 1024, 1024], P(None, 'tp', 'fsdp')
- new_fc1: float32 [2, 1024, 4096], P(None, 'fsdp', 'tp')
- new_fc2: float32 [2, 4096, 1024], P(None, 'tp', 'fsdp')
- new_mom_query: float32 [2, 1024, 1024], P(None, 'fsdp', 'tp')
- new_mom_key: float32 [2, 1024, 1024], P(None, 'fsdp', 'tp')
- new_mom_value: float32 [2, 1024, 1024], P(None, 'fsdp', 'tp')
- new_mom_out: float32 [2, 1024, 1024], P(None, 'tp', 'fsdp')
- new_mom_fc1: float32 [2, 1024, 4096], P(None, 'fsdp', 'tp')
- new_mom_fc2: float32 [2, 4096, 1024], P(None, 'tp', 'fsdp')
- new_vectors: float32 [2, 8, 1024], replicated
- new_fc1_bias: float32 [2, 4096], replicated
- new_vec_first: float32 [2, 8, 1024], replicated
- new_vec_second: float32 [2, 8, 1024], replicated
- new_bias_first: float32 [2, 4096], replicated
- new_bias_second: float32 [2, 4096], replicated
The draws below stay inside these ranges and needn't reach their ends.
Inputs may be any that keep to these rules, and one draw needn't show every extreme that they name: `vectors`: rows 0 and 5 of each block lie in 0.7 to 1.3; the other rows in -1 to 1.
All inputs are finite; a program needn't handle non-finite values.
Results may differ from the reference program's by a relative error of at most 0.029.
Values may be sent and summed in bfloat16 or wider, within the bound.
No kernel may reach another device: no remote copies, remote signals or barrier semaphores. Data moves between devices by JAX's collectives and lax.ppermute only.
A program may use at most 192 MiB of HBM per device.

```python
import math
import jax
import jax.numpy as jnp
from jax import lax

D = 1024
HEADS = 16
HEAD_DIM = 64
FF = 4096
SEQ = 577
LAYERS = 2
NS_ITERS = 3
IMAGES = 8
N_TP = 4


def draw_vectors(key, part):
    base_key, gain_key = jax.random.split(jax.random.fold_in(key, 11))
    shape = (LAYERS, 8, D)
    spread = jnp.clip(0.4 * jax.random.normal(base_key, shape, jnp.float32), -1.0, 1.0)
    wobble = jnp.clip(jax.random.normal(gain_key, shape, jnp.float32), -3.0, 3.0) / 3.0
    slot = lax.broadcasted_iota(jnp.int32, shape, 1)
    is_gain = (slot == 0) | (slot == 5)
    return jnp.where(is_gain, 1.0 + 0.3 * wobble, spread).astype(jnp.float32)


def level_of(rng, dims, cuts, smallest, largest):
    level, own = 1.0, jax.random.fold_in(rng, 6)
    for dim, shards_of in cuts:
        steps = jnp.exp(jax.random.uniform(jax.random.fold_in(own, dim), (shards_of,), jnp.float32, smallest / len(cuts), largest / len(cuts)))
        level = level * jnp.repeat(steps, dims[dim] // shards_of).reshape([-1 if axis == dim else 1 for axis in range(len(dims))])
    return level


def scatter_about(own_key, dims, width, bound, cuts=(), dtype=jnp.bfloat16):
    values = width * jax.random.normal(own_key, dims, jnp.float32)
    if cuts:
        values = values * level_of(own_key, dims, cuts, -0.22, 0.18)
    return jnp.clip(values, -bound, bound).astype(dtype)


def setup_inputs(seed: int = 0) -> dict:
    streams_of = jax.random.split(jax.random.key(seed), 21)
    return {
        "tokens_in": scatter_about(streams_of[0], (IMAGES, SEQ, D), 1.0, 6.0, ((0, 8),)),
        "cotangent": scatter_about(streams_of[1], (IMAGES, SEQ, D), 1.0, 6.0, ((0, 8),)),
        "w_query": scatter_about(streams_of[2], (LAYERS, D, D), D ** -0.5, 0.1875, ((1, 8), (2, 4)), jnp.float32),
        "w_key": scatter_about(streams_of[3], (LAYERS, D, D), D ** -0.5, 0.1875, ((1, 8), (2, 4)), jnp.float32),
        "w_value": scatter_about(streams_of[4], (LAYERS, D, D), D ** -0.5, 0.1875, ((1, 8), (2, 4)), jnp.float32),
        "w_out": scatter_about(streams_of[5], (LAYERS, D, D), (max(D // 8, 1)) ** -0.5, 0.5, ((1, 4), (2, 8)), jnp.float32),
        "w_fc1": scatter_about(streams_of[6], (LAYERS, D, FF), D ** -0.5, 0.1875, ((1, 8), (2, 4)), jnp.float32),
        "w_fc2": scatter_about(streams_of[7], (LAYERS, FF, D), FF ** -0.5, 0.09375, ((1, 4), (2, 8)), jnp.float32),
        "mom_query": scatter_about(streams_of[8], (LAYERS, D, D), 8.0, 48.0, ((1, 8), (2, 4)), jnp.float32),
        "mom_key": scatter_about(streams_of[9], (LAYERS, D, D), 8.0, 48.0, ((1, 8), (2, 4)), jnp.float32),
        "mom_value": scatter_about(streams_of[10], (LAYERS, D, D), 40.0, 256.0, ((1, 8), (2, 4)), jnp.float32),
        "mom_out": scatter_about(streams_of[11], (LAYERS, D, D), 20.0, 128.0, ((1, 4), (2, 8)), jnp.float32),
        "mom_fc1": scatter_about(streams_of[12], (LAYERS, D, FF), 20.0, 128.0, ((1, 8), (2, 4)), jnp.float32),
        "mom_fc2": scatter_about(streams_of[13], (LAYERS, FF, D), 40.0, 256.0, ((1, 4), (2, 8)), jnp.float32),
        "vectors": draw_vectors(jax.random.fold_in(streams_of[20], 71), 0),
        "fc1_bias": scatter_about(streams_of[15], (LAYERS, FF), 0.5, 3.0, (), jnp.float32),
        "vec_first": scatter_about(streams_of[16], (LAYERS, 8, D), 6.0, 32.0, (), jnp.float32),
        "vec_second": jnp.clip(jnp.exp(jax.random.uniform(streams_of[17], (LAYERS, 8, D), jnp.float32, math.log(20.0), math.log(400.0))), 20.0, 400.0),
        "bias_first": scatter_about(streams_of[18], (LAYERS, FF), 3.0, 16.0, (), jnp.float32),
        "bias_second": jnp.clip(jnp.exp(jax.random.uniform(streams_of[19], (LAYERS, FF), jnp.float32, math.log(5.0), math.log(100.0))), 5.0, 100.0),
    }


coef_first = 3.4445
coef_second = -4.775
coef_third = 2.0315
muon_beta = 0.95
muon_rate = 0.1
muon_decay = 0.1
adam_rate = 0.05
adam_first = 0.9
adam_second = 0.95
adam_eps = 1e-08
adam_count = 3.0
norm_eps = 1e-06

def rounded(value):
    return value.astype(jnp.bfloat16)

def widened(value):
    return value.astype(jnp.float32)

def layer_norm(hidden, gain, shift):
    centred = hidden - lax.optimization_barrier(jnp.mean(hidden, axis=-1, keepdims=True))
    inverse = lax.rsqrt(lax.optimization_barrier(jnp.mean(centred * centred, axis=-1, keepdims=True)) + norm_eps)
    normed = centred * inverse
    return (normed * gain + shift, normed, inverse)

def norm_back(grad_out, normed, inverse, gain):
    scaled = grad_out * gain
    return inverse * (scaled - lax.optimization_barrier(jnp.mean(scaled, axis=-1, keepdims=True)) - normed * lax.optimization_barrier(jnp.mean(scaled * normed, axis=-1, keepdims=True)))

def gelu_exact(value):
    return jax.nn.gelu(value, approximate=False)

def group_sum(pairs):
    total = None
    for left, right in pairs:
        term = jnp.einsum('spk,pkd->psd', widened(left).reshape(left.shape[0], N_TP, -1), widened(right).reshape(N_TP, -1, right.shape[1]))
        total = term if total is None else total + term
    return lax.optimization_barrier(jnp.sum(widened(rounded(total)), axis=0))

def newton(wide):
    wide_low = rounded(wide)
    total = jnp.sum(widened(wide_low) * widened(wide_low))
    factor = 1.0 / (jnp.sqrt(total) + norm_eps)
    iterate = rounded(widened(wide_low) * factor)
    for step in range(NS_ITERS):
        groups = widened(iterate).reshape(wide.shape[0], N_TP, -1)
        gram = lax.optimization_barrier(jnp.sum(widened(rounded(jnp.einsum('dpc,epc->pde', groups, groups))), axis=0))
        gram_low = rounded(gram)
        poly_low = rounded(coef_second * gram + coef_third * jnp.dot(gram_low, gram_low, preferred_element_type=jnp.float32))
        iterate = rounded(coef_first * widened(iterate) + jnp.dot(poly_low, iterate, preferred_element_type=jnp.float32))
    return widened(iterate)

def adam(param, first, second, grad):
    new_first = adam_first * first + (1.0 - adam_first) * grad
    new_second = adam_second * second + (1.0 - adam_second) * grad * grad
    first_hat = new_first / (1.0 - adam_first ** adam_count)
    second_hat = new_second / (1.0 - adam_second ** adam_count)
    return (param - adam_rate * first_hat / (jnp.sqrt(second_hat) + adam_eps), new_first, new_second)

def muon(weight, moment, grad, flip):
    new_moment = muon_beta * moment + grad
    nest = grad + muon_beta * new_moment
    wide = nest.T if flip else nest
    ortho = newton(wide)
    update = ortho.T if flip else ortho
    new_weight = weight * (1.0 - muon_rate * muon_decay) - muon_rate * 0.2 * math.sqrt(wide.shape[1]) * update
    return (new_weight, new_moment)

def reference(tokens_in, cotangent, w_query, w_key, w_value, w_out, w_fc1, w_fc2, mom_query, mom_key, mom_value, mom_out, mom_fc1, mom_fc2, vectors, fc1_bias, vec_first, vec_second, bias_first, bias_second):
    wq_low, wk_low, wv_low, wo_low, w1_low, w2_low = [rounded(item) for item in (w_query, w_key, w_value, w_out, w_fc1, w_fc2)]
    scale = 1.0 / math.sqrt(HEAD_DIM)

    def heads(flat):
        return widened(flat).reshape(SEQ, HEADS, HEAD_DIM)

    def image_pass(totals, item):
        image_in, image_cot = item
        total_query, total_key, total_value, total_out, total_fc1, total_fc2, total_vec, total_bias = totals
        hidden = widened(image_in)
        kept = []
        for layer in range(LAYERS):
            gains = vectors[layer]
            normed_in, hat_one, inverse_one = layer_norm(hidden, gains[0], gains[1])
            attn_in = rounded(normed_in)
            query_low = rounded(jnp.dot(attn_in, wq_low[layer], preferred_element_type=jnp.float32) + gains[2])
            key_low = rounded(jnp.dot(attn_in, wk_low[layer], preferred_element_type=jnp.float32))
            value_low = rounded(jnp.dot(attn_in, wv_low[layer], preferred_element_type=jnp.float32) + gains[3])
            scores = jnp.einsum('qhd,khd->hqk', heads(query_low), heads(key_low)) * scale
            log_total = jnp.log(lax.optimization_barrier(jnp.sum(jnp.exp(scores), axis=-1)))
            probs_low = rounded(jnp.exp(scores - log_total[..., None]))
            context_low = rounded(jnp.einsum('hqk,khd->qhd', widened(probs_low), heads(value_low))).reshape(SEQ, D)
            after = hidden + group_sum([(context_low, wo_low[layer])]) + gains[4]
            normed_mid, hat_two, inverse_two = layer_norm(after, gains[5], gains[6])
            mid_low = rounded(normed_mid)
            preact = jnp.dot(mid_low, w1_low[layer], preferred_element_type=jnp.float32) + fc1_bias[layer]
            up_low = rounded(gelu_exact(preact))
            kept.append((hat_one, inverse_one, attn_in, query_low, key_low, value_low, log_total, context_low, hat_two, inverse_two, mid_low, preact, up_low))
            hidden = after + group_sum([(up_low, w2_low[layer])]) + gains[7]
        image_out = rounded(hidden)
        grad = widened(image_cot)
        for layer in reversed(range(LAYERS)):
            hat_one, inverse_one, attn_in, query_low, key_low, value_low, log_total, context_low, hat_two, inverse_two, mid_low, preact, up_low = kept[layer]
            gains = vectors[layer]
            grad_low = rounded(grad)
            total_fc2 = total_fc2.at[layer].add(jnp.dot(up_low.T, grad_low, preferred_element_type=jnp.float32))
            d_up = jnp.dot(grad_low, w2_low[layer].T, preferred_element_type=jnp.float32)
            unused, gelu_back = jax.vjp(gelu_exact, preact)
            d_pre = gelu_back(d_up)[0]
            pre_low = rounded(d_pre)
            total_fc1 = total_fc1.at[layer].add(jnp.dot(mid_low.T, pre_low, preferred_element_type=jnp.float32))
            d_mid = group_sum([(pre_low, w1_low[layer].T)])
            grad_after = grad + norm_back(d_mid, hat_two, inverse_two, gains[5])
            after_low = rounded(grad_after)
            total_out = total_out.at[layer].add(jnp.dot(context_low.T, after_low, preferred_element_type=jnp.float32))
            d_context = widened(rounded(jnp.dot(after_low, wo_low[layer].T, preferred_element_type=jnp.float32))).reshape(SEQ, HEADS, HEAD_DIM)
            query_heads = heads(query_low)
            key_heads = heads(key_low)
            scores = jnp.einsum('qhd,khd->hqk', query_heads, key_heads) * scale
            probs = jnp.exp(scores - log_total[..., None])
            d_probs = jnp.einsum('qhd,khd->hqk', d_context, heads(value_low))
            d_value = jnp.einsum('hqk,qhd->khd', widened(rounded(probs)), d_context).reshape(SEQ, D)
            delta = lax.optimization_barrier(jnp.sum(probs * d_probs, axis=-1, keepdims=True))
            d_scores = widened(rounded(probs * (d_probs - delta) * scale))
            d_query = jnp.einsum('hqk,khd->qhd', d_scores, key_heads).reshape(SEQ, D)
            d_key = jnp.einsum('hqk,qhd->khd', d_scores, query_heads).reshape(SEQ, D)
            query_grad_low = rounded(d_query)
            key_grad_low = rounded(d_key)
            value_grad_low = rounded(d_value)
            total_query = total_query.at[layer].add(jnp.dot(attn_in.T, query_grad_low, preferred_element_type=jnp.float32))
            total_key = total_key.at[layer].add(jnp.dot(attn_in.T, key_grad_low, preferred_element_type=jnp.float32))
            total_value = total_value.at[layer].add(jnp.dot(attn_in.T, value_grad_low, preferred_element_type=jnp.float32))
            d_in = group_sum([(query_grad_low, wq_low[layer].T), (key_grad_low, wk_low[layer].T), (value_grad_low, wv_low[layer].T)])
            rows = jnp.stack([lax.optimization_barrier(jnp.sum(d_in * hat_one, axis=0)), lax.optimization_barrier(jnp.sum(d_in, axis=0)), lax.optimization_barrier(jnp.sum(d_query, axis=0)), lax.optimization_barrier(jnp.sum(d_value, axis=0)), lax.optimization_barrier(jnp.sum(grad_after, axis=0)), lax.optimization_barrier(jnp.sum(d_mid * hat_two, axis=0)), lax.optimization_barrier(jnp.sum(d_mid, axis=0)), lax.optimization_barrier(jnp.sum(grad, axis=0))])
            total_vec = total_vec.at[layer].add(rows)
            total_bias = total_bias.at[layer].add(lax.optimization_barrier(jnp.sum(d_pre, axis=0)))
            grad = grad_after + norm_back(d_in, hat_one, inverse_one, gains[0])
        return ((total_query, total_key, total_value, total_out, total_fc1, total_fc2, total_vec, total_bias), (image_out, grad))
    start = (jnp.zeros((LAYERS, D, D), jnp.float32), jnp.zeros((LAYERS, D, D), jnp.float32), jnp.zeros((LAYERS, D, D), jnp.float32), jnp.zeros((LAYERS, D, D), jnp.float32), jnp.zeros((LAYERS, D, FF), jnp.float32), jnp.zeros((LAYERS, FF, D), jnp.float32), jnp.zeros((LAYERS, 8, D), jnp.float32), jnp.zeros((LAYERS, FF), jnp.float32))
    totals, outputs = lax.scan(image_pass, start, (tokens_in, cotangent))
    grad_query, grad_key, grad_value, grad_out, grad_fc1, grad_fc2, grad_vectors, grad_fc1_bias = totals
    tokens_out, input_grad = outputs
    weights = (w_query, w_key, w_value, w_out, w_fc1, w_fc2)
    moments = (mom_query, mom_key, mom_value, mom_out, mom_fc1, mom_fc2)
    grads = (grad_query, grad_key, grad_value, grad_out, grad_fc1, grad_fc2)
    flips = (False, False, False, True, False, True)
    new_weights = []
    new_moments = []
    for index in range(6):
        layer_weights = []
        layer_moments = []
        for layer in range(LAYERS):
            weight_new, moment_new = muon(weights[index][layer], moments[index][layer], grads[index][layer], flips[index])
            layer_weights.append(weight_new)
            layer_moments.append(moment_new)
        new_weights.append(jnp.stack(layer_weights))
        new_moments.append(jnp.stack(layer_moments))
    new_vectors, new_vec_first, new_vec_second = adam(vectors, vec_first, vec_second, grad_vectors)
    new_fc1_bias, new_bias_first, new_bias_second = adam(fc1_bias, bias_first, bias_second, grad_fc1_bias)
    return (tokens_out, input_grad, grad_query, grad_key, grad_value, grad_out, grad_fc1, grad_fc2, grad_vectors, grad_fc1_bias, new_weights[0], new_weights[1], new_weights[2], new_weights[3], new_weights[4], new_weights[5], new_moments[0], new_moments[1], new_moments[2], new_moments[3], new_moments[4], new_moments[5], new_vectors, new_fc1_bias, new_vec_first, new_vec_second, new_bias_first, new_bias_second)
```

```python
import math

import jax
import jax.numpy as jnp
from jax import lax
from jax.sharding import PartitionSpec as P

D = 1024
HEAD_DIM = 64
FF = 4096
LAYERS = 2
NS_ITERS = 3


coef_first = 3.4445
coef_second = -4.775
coef_third = 2.0315
muon_beta = 0.95
muon_rate = 0.1
muon_decay = 0.1
adam_rate = 0.05
adam_first = 0.9
adam_second = 0.95
adam_eps = 1e-08
adam_count = 3.0
norm_eps = 1e-06


def rounded(value):
    return value.astype(jnp.bfloat16)


def widened(value):
    return value.astype(jnp.float32)


def layer_norm(hidden, gain, shift):
    centred = hidden - jnp.mean(hidden, axis=-1, keepdims=True)
    inverse = lax.rsqrt(jnp.mean(centred * centred, axis=-1, keepdims=True) + norm_eps)
    normed = centred * inverse
    return (normed * gain + shift, normed, inverse)


def norm_back(grad_out, normed, inverse, gain):
    scaled = grad_out * gain
    return inverse * (
        scaled
        - jnp.mean(scaled, axis=-1, keepdims=True)
        - normed * jnp.mean(scaled * normed, axis=-1, keepdims=True)
    )


def gelu_exact(value):
    return jax.nn.gelu(value, approximate=False)


def adam(param, first, second, grad):
    new_first = adam_first * first + (1.0 - adam_first) * grad
    new_second = adam_second * second + (1.0 - adam_second) * grad * grad
    first_hat = new_first / (1.0 - adam_first**adam_count)
    second_hat = new_second / (1.0 - adam_second**adam_count)
    return (
        param - adam_rate * first_hat / (jnp.sqrt(second_hat) + adam_eps),
        new_first,
        new_second,
    )


def inner_rows(left, right):
    return lax.dot_general(
        left, right, (((0,), (0,)), ((), ())), preferred_element_type=jnp.float32
    )


def times_trans(left, right):
    return lax.dot_general(
        left, right, (((1,), (1,)), ((), ())), preferred_element_type=jnp.float32
    )


def product(left, right):
    return jnp.dot(left, right, preferred_element_type=jnp.float32)


def ring_order(count):
    outer = 4
    inner = count // outer
    if count % outer or inner < 2:
        return list(range(count))
    walk = []
    for row in range(outer):
        columns = range(1, inner) if row % 2 == 0 else range(inner - 1, 0, -1)
        walk += [row * inner + column for column in columns]
    return walk + [row * inner for row in range(outer - 1, -1, -1)]


class Layout:
    def __init__(self):
        self.fsdp = lax.axis_size("fsdp")
        self.tp = lax.axis_size("tp")
        self.rank = lax.axis_index("fsdp")
        self.slot = lax.axis_index("tp")
        walk = ring_order(self.fsdp)
        place = {rank: at for at, rank in enumerate(walk)}
        table = [
            [walk[(place[rank] + step) % self.fsdp] for step in range(self.fsdp)]
            for rank in range(self.fsdp)
        ]
        self.ahead = jnp.asarray(table, jnp.int32)[self.rank]
        self.forward = [(row[0], row[1]) for row in table]
        self.backward = [(row[0], row[-1]) for row in table]

    def at(self, step):
        return self.ahead[step % self.fsdp]

    def send_forward(self, value):
        return lax.ppermute(value, "fsdp", self.forward)

    def send_backward(self, value):
        return lax.ppermute(value, "fsdp", self.backward)

    def swap_tp(self, value, bit):
        return lax.ppermute(value, "tp", [(at, at ^ bit) for at in range(self.tp)])

    def gather(self, piece):
        rows, columns = piece.shape
        half = columns // 2
        reach = self.fsdp // 2
        whole = jnp.zeros((self.fsdp * rows, columns), piece.dtype)
        whole = lax.dynamic_update_slice(whole, piece, (self.rank * rows, 0))
        fore = back = piece
        for step in range(1, reach):
            fore = self.send_forward(fore)
            back = self.send_backward(back)
            whole = lax.dynamic_update_slice(whole, fore, (self.at(-step) * rows, 0))
            whole = lax.dynamic_update_slice(whole, back, (self.at(step) * rows, 0))
        fore = self.send_forward(fore[:, :half])
        back = self.send_backward(back[:, half:])
        last = self.at(reach) * rows
        whole = lax.dynamic_update_slice(whole, fore, (last, 0))
        return lax.dynamic_update_slice(whole, back, (last, half))

    def scatter_sum(self, parts):
        rows, columns = parts.shape[0] // self.fsdp, parts.shape[1]
        half = columns // 2
        reach = self.fsdp // 2

        def own(step):
            return lax.dynamic_slice(parts, (self.at(step) * rows, 0), (rows, columns))

        far = own(reach)
        fore = self.send_forward(far[:, :half])
        back = self.send_backward(far[:, half:])
        for step in range(reach - 1, 0, -1):
            mine_fore, mine_back = own(step), own(-step)
            if step == reach - 1:
                fore = jnp.concatenate([mine_fore[:, :half] + fore, mine_fore[:, half:]], axis=1)
                back = jnp.concatenate([mine_back[:, :half], mine_back[:, half:] + back], axis=1)
            else:
                fore = mine_fore + fore
                back = mine_back + back
            fore = self.send_forward(fore)
            back = self.send_backward(back)
        return widened(own(0)) + widened(fore) + widened(back)

    def tp_sum(self, term):
        half = term.shape[1] // 2
        core = self.slot % 2
        low = rounded(term)
        mine = lax.dynamic_slice_in_dim(low, core * half, half, 1)
        other = lax.dynamic_slice_in_dim(low, (1 - core) * half, half, 1)
        total = rounded(widened(mine) + widened(self.swap_tp(other, 1)))
        bit = 2
        while bit < self.tp:
            total = rounded(widened(total) + widened(self.swap_tp(total, bit)))
            bit *= 2
        other = self.swap_tp(total, 1)
        first = jnp.where(core == 0, total, other)
        second = jnp.where(core == 0, other, total)
        return widened(jnp.concatenate([first, second], axis=1))

    def mesh_sum(self, value):
        bit = 1
        while bit < self.tp:
            value = value + self.swap_tp(value, bit)
            bit *= 2
        bit = 1
        while bit < self.fsdp:
            pairs = [(at, at ^ bit) for at in range(self.fsdp)]
            value = value + lax.ppermute(value, "fsdp", pairs)
            bit *= 2
        return value

    def owners(self):
        part = max(self.fsdp // 8, 1)
        return [rank * part % self.fsdp for rank in (3, 2, 5, 4, 1, 6)]

    def kind_table(self, kinds):
        table = [0] * self.fsdp
        for index, kind in enumerate(kinds):
            table[self.owners()[kind]] = index
        return jnp.asarray(table, jnp.int32)

    def collect(self, stack, kinds):
        count, rows, columns = stack.shape
        owning = {self.owners()[kind] for kind in kinds}
        table = self.kind_table(kinds)

        def pick(target):
            return lax.dynamic_index_in_dim(stack, table[target], 0, keepdims=False)

        tile = jnp.zeros((self.fsdp * rows, columns), stack.dtype)
        tile = lax.dynamic_update_slice(tile, pick(self.rank), (self.rank * rows, 0))
        for shift in range(1, self.fsdp):
            pairs = [
                (at, (at + shift) % self.fsdp)
                for at in range(self.fsdp)
                if (at + shift) % self.fsdp in owning
            ]
            got = lax.ppermute(pick((self.rank + shift) % self.fsdp), "fsdp", pairs)
            source = (self.rank - shift) % self.fsdp
            tile = lax.dynamic_update_slice(tile, got, (source * rows, 0))
        return tile

    def give_back(self, tile, kinds):
        rows, columns = tile.shape[0] // self.fsdp, tile.shape[1]
        owning = {self.owners()[kind] for kind in kinds}
        spare = len(kinds)
        table = [spare] * self.fsdp
        for index, kind in enumerate(kinds):
            table[self.owners()[kind]] = index
        table = jnp.asarray(table, jnp.int32)

        def rows_of(rank):
            return lax.dynamic_slice(tile, (rank * rows, 0), (rows, columns))

        out = jnp.zeros((spare + 1, rows, columns), tile.dtype)
        out = lax.dynamic_update_slice(out, rows_of(self.rank)[None], (table[self.rank], 0, 0))
        for shift in range(1, self.fsdp):
            pairs = [
                (at, (at + shift) % self.fsdp) for at in range(self.fsdp) if at in owning
            ]
            got = lax.ppermute(rows_of((self.rank + shift) % self.fsdp), "fsdp", pairs)
            source = table[(self.rank - shift) % self.fsdp]
            out = lax.dynamic_update_slice(out, got[None], (source, 0, 0))
        return out[:spare]

    def matrix_of_slot(self):
        step = max(self.tp // 4, 1)
        return [at // step if at % step == 0 and at // step < 4 else -1 for at in range(self.tp)]

    def att_out(self, packed):
        rows, columns = packed.shape[0], packed.shape[1] // 4
        held = self.matrix_of_slot()
        table = jnp.asarray([max(item, 0) for item in held], jnp.int32)

        def pick(target):
            return lax.dynamic_slice(packed, (0, table[target] * columns), (rows, columns))

        whole = jnp.zeros((rows, self.tp * columns), packed.dtype)
        whole = lax.dynamic_update_slice(whole, pick(self.slot), (0, self.slot * columns))
        for mask in range(1, self.tp):
            pairs = [(at, at ^ mask) for at in range(self.tp) if held[at ^ mask] >= 0]
            got = lax.ppermute(pick(self.slot ^ mask), "tp", pairs)
            whole = lax.dynamic_update_slice(whole, got, (0, (self.slot ^ mask) * columns))
        return whole

    def att_back(self, whole):
        rows, columns = whole.shape[0], whole.shape[1] // self.tp
        held = self.matrix_of_slot()
        table = jnp.asarray([item if item >= 0 else 4 for item in held], jnp.int32)

        def part(target):
            return lax.dynamic_slice(whole, (0, target * columns), (rows, columns))

        packed = jnp.zeros((rows, 5 * columns), whole.dtype)
        packed = lax.dynamic_update_slice(packed, part(self.slot), (0, table[self.slot] * columns))
        for mask in range(1, self.tp):
            pairs = [(at, at ^ mask) for at in range(self.tp) if held[at] >= 0]
            got = lax.ppermute(part(self.slot ^ mask), "tp", pairs)
            at = table[self.slot ^ mask] * columns
            packed = lax.dynamic_update_slice(packed, got, (0, at))
        return packed[:, : 4 * columns]


def solve_square(tile):
    total = jnp.sum(jnp.square(widened(tile)))
    iterate = rounded(widened(tile) * (1.0 / (jnp.sqrt(total) + norm_eps)))
    for step in range(NS_ITERS):
        gram = times_trans(iterate, iterate)
        gram_low = rounded(gram)
        poly = rounded(coef_second * gram + coef_third * product(gram_low, gram_low))
        iterate = rounded(coef_first * widened(iterate) + product(poly, iterate))
    return iterate


def solve_wide(tile, gram_raw):
    size = gram_raw.shape[0]
    on_diagonal = lax.broadcasted_iota(jnp.int32, (size, size), 0) == lax.broadcasted_iota(
        jnp.int32, (size, size), 1
    )
    total = jnp.sum(jnp.where(on_diagonal, gram_raw, 0.0))
    factor = 1.0 / (jnp.sqrt(total) + norm_eps)
    start = rounded(widened(tile) * factor)
    gram = gram_raw * (factor * factor)
    rest = None
    lead = 1.0
    for step in range(NS_ITERS):
        gram_low = rounded(gram)
        poly = rounded(coef_second * gram + coef_third * product(gram_low, gram_low))
        if rest is None:
            rest = poly
        else:
            rest = rounded(
                coef_first * widened(rest) + lead * widened(poly) + product(poly, rest)
            )
        lead = lead * coef_first
        if step + 1 < NS_ITERS:
            half = coef_first * gram + product(gram_low, poly)
            gram = coef_first * half + product(poly, rounded(half))
    return rounded(lead * widened(start) + product(rest, start))


def flip(stack):
    return jnp.swapaxes(stack, 1, 2)


def per_device(
    tokens_in,
    cotangent,
    w_query,
    w_key,
    w_value,
    w_out,
    w_fc1,
    w_fc2,
    mom_query,
    mom_key,
    mom_value,
    mom_out,
    mom_fc1,
    mom_fc2,
    vectors,
    fc1_bias,
    vec_first,
    vec_second,
    bias_first,
    bias_second,
):
    spot = Layout()
    tp_count = spot.tp
    tp_at = spot.slot
    leading = (tp_at == 0).astype(jnp.float32)
    images = tokens_in.shape[0]
    seq_len = tokens_in.shape[1]
    width = tokens_in.shape[2]
    rows = images * seq_len
    att_cols = w_query.shape[2]
    ff_cols = w_fc1.shape[2]
    heads_here = att_cols // HEAD_DIM
    scale = 1.0 / math.sqrt(HEAD_DIM)

    def pack_att(query, key, value, out):
        return jnp.concatenate([query, key, value, flip(out)], axis=2)

    att_low = rounded(pack_att(w_query, w_key, w_value, w_out))
    fc1_low = rounded(w_fc1)
    fc2_low = rounded(flip(w_fc2))
    att_all, fc1_all, fc2_all = [], [], []
    for layer in range(LAYERS):
        att_all.append(spot.gather(att_low[layer]))
        fc1_all.append(spot.gather(fc1_low[layer]))
        fc2_all.append(spot.gather(fc2_low[layer]))

    def heads(flat):
        return flat.reshape(images, seq_len, heads_here, HEAD_DIM)

    hidden = widened(tokens_in.reshape(rows, width))
    kept = []
    for layer in range(LAYERS):
        gains = vectors[layer]
        qkv_all, out_all = att_all[layer][:, : 3 * att_cols], att_all[layer][:, 3 * att_cols :]
        normed_in, hat_one, inverse_one = layer_norm(hidden, gains[0], gains[1])
        attn_in = rounded(normed_in)
        query_shift = lax.dynamic_slice_in_dim(gains[2], tp_at * att_cols, att_cols)
        value_shift = lax.dynamic_slice_in_dim(gains[3], tp_at * att_cols, att_cols)
        shift = jnp.concatenate([query_shift, jnp.zeros_like(query_shift), value_shift])
        qkv_low = rounded(product(attn_in, qkv_all) + shift)
        query_low, key_low, value_low = jnp.split(qkv_low, 3, axis=1)
        scores = (
            jnp.einsum(
                "bqhd,bkhd->bhqk",
                heads(query_low),
                heads(key_low),
                preferred_element_type=jnp.float32,
            )
            * scale
        )
        log_total = jnp.log(jnp.sum(jnp.exp(scores), axis=-1))
        probs_low = rounded(jnp.exp(scores - log_total[..., None]))
        context_low = rounded(
            jnp.einsum(
                "bhqk,bkhd->bqhd", probs_low, heads(value_low), preferred_element_type=jnp.float32
            )
        ).reshape(rows, att_cols)
        after = hidden + spot.tp_sum(times_trans(context_low, out_all)) + gains[4]
        normed_mid, hat_two, inverse_two = layer_norm(after, gains[5], gains[6])
        mid_low = rounded(normed_mid)
        fc1_shift = lax.dynamic_slice_in_dim(fc1_bias[layer], tp_at * ff_cols, ff_cols)
        preact = product(mid_low, fc1_all[layer]) + fc1_shift
        up_low = rounded(gelu_exact(preact))
        kept.append(
            (
                hat_one,
                inverse_one,
                attn_in,
                query_low,
                key_low,
                value_low,
                log_total,
                context_low,
                hat_two,
                inverse_two,
                mid_low,
                preact,
                up_low,
            )
        )
        hidden = after + spot.tp_sum(times_trans(up_low, fc2_all[layer])) + gains[7]
    tokens_out = rounded(hidden).reshape(images, seq_len, width)
    grad = widened(cotangent.reshape(rows, width))
    sum_att = [None] * LAYERS
    sum_fc1 = [None] * LAYERS
    sum_fc2 = [None] * LAYERS
    part_vec = [None] * LAYERS
    zero_row = jnp.zeros((width,), jnp.float32)
    zero_hidden = jnp.zeros((fc1_bias.shape[1],), jnp.float32)
    for layer in reversed(range(LAYERS)):
        (
            hat_one,
            inverse_one,
            attn_in,
            query_low,
            key_low,
            value_low,
            log_total,
            context_low,
            hat_two,
            inverse_two,
            mid_low,
            preact,
            up_low,
        ) = kept[layer]
        gains = vectors[layer]
        qkv_all, out_all = att_all[layer][:, : 3 * att_cols], att_all[layer][:, 3 * att_cols :]
        grad_low = rounded(grad)
        sum_fc2[layer] = spot.scatter_sum(rounded(inner_rows(grad_low, up_low)))
        d_up = product(grad_low, fc2_all[layer])
        unused, gelu_back = jax.vjp(gelu_exact, preact)
        d_pre = gelu_back(d_up)[0]
        pre_low = rounded(d_pre)
        sum_fc1[layer] = spot.scatter_sum(rounded(inner_rows(mid_low, pre_low)))
        d_mid = spot.tp_sum(times_trans(pre_low, fc1_all[layer]))
        grad_after = grad + norm_back(d_mid, hat_two, inverse_two, gains[5])
        after_low = rounded(grad_after)
        d_context = heads(rounded(product(after_low, out_all)))
        query_heads = heads(query_low)
        key_heads = heads(key_low)
        scores = (
            jnp.einsum(
                "bqhd,bkhd->bhqk", query_heads, key_heads, preferred_element_type=jnp.float32
            )
            * scale
        )
        probs = jnp.exp(scores - log_total[..., None])
        d_probs = jnp.einsum(
            "bqhd,bkhd->bhqk", d_context, heads(value_low), preferred_element_type=jnp.float32
        )
        d_value = jnp.einsum(
            "bhqk,bqhd->bkhd", rounded(probs), d_context, preferred_element_type=jnp.float32
        ).reshape(rows, att_cols)
        delta = jnp.sum(probs * d_probs, axis=-1, keepdims=True)
        d_scores = rounded(probs * (d_probs - delta) * scale)
        d_query = jnp.einsum(
            "bhqk,bkhd->bqhd", d_scores, key_heads, preferred_element_type=jnp.float32
        ).reshape(rows, att_cols)
        d_key = jnp.einsum(
            "bhqk,bqhd->bkhd", d_scores, query_heads, preferred_element_type=jnp.float32
        ).reshape(rows, att_cols)
        d_qkv_low = rounded(jnp.concatenate([d_query, d_key, d_value], axis=1))
        part_att = jnp.concatenate(
            [
                rounded(inner_rows(attn_in, d_qkv_low)),
                rounded(inner_rows(after_low, context_low)),
            ],
            axis=1,
        )
        sum_att[layer] = spot.scatter_sum(part_att)
        d_in = spot.tp_sum(times_trans(d_qkv_low, qkv_all))
        row_query = lax.dynamic_update_slice_in_dim(
            zero_row, jnp.sum(d_query, axis=0), tp_at * att_cols, 0
        )
        row_value = lax.dynamic_update_slice_in_dim(
            zero_row, jnp.sum(d_value, axis=0), tp_at * att_cols, 0
        )
        bias_row = lax.dynamic_update_slice_in_dim(
            zero_hidden, jnp.sum(d_pre, axis=0), tp_at * ff_cols, 0
        )
        part_vec[layer] = jnp.concatenate(
            [
                jnp.stack(
                    [
                        leading * jnp.sum(d_in * hat_one, axis=0),
                        leading * jnp.sum(d_in, axis=0),
                        row_query,
                        row_value,
                        leading * jnp.sum(grad_after, axis=0),
                        leading * jnp.sum(d_mid * hat_two, axis=0),
                        leading * jnp.sum(d_mid, axis=0),
                        leading * jnp.sum(grad, axis=0),
                    ]
                ),
                bias_row.reshape(-1, width),
            ],
            axis=0,
        )
        grad = grad_after + norm_back(d_in, hat_one, inverse_one, gains[0])
    input_grad = grad.reshape(images, seq_len, width)
    vec_rows = vectors.shape[1]
    sums = spot.mesh_sum(jnp.stack(part_vec))
    grad_vectors = sums[:, :vec_rows]
    grad_fc1_bias = sums[:, vec_rows:].reshape(LAYERS, -1)

    mom_att = pack_att(mom_query, mom_key, mom_value, mom_out)
    mom_fc2_flip = flip(mom_fc2)

    def nest_of(gradient, moment):
        return rounded(gradient + muon_beta * (muon_beta * moment + gradient))

    tile_cols = max(tp_count * att_cols, ff_cols)

    def widen_tile(piece):
        return jnp.pad(piece, ((0, 0), (0, tile_cols - piece.shape[1])))

    tiles = []
    for layer in range(LAYERS):
        tiles += [
            spot.att_out(nest_of(sum_att[layer], mom_att[layer])),
            widen_tile(nest_of(sum_fc1[layer], mom_fc1[layer])),
            widen_tile(nest_of(sum_fc2[layer], mom_fc2_flip[layer])),
        ]
    kinds = list(range(3 * LAYERS))
    tile = spot.collect(jnp.stack(tiles), kinds)
    gram = spot.tp_sum(times_trans(tile, tile))
    roles = [0] * spot.fsdp
    for kind, rank in enumerate(spot.owners()):
        roles[rank] = 1 if kind % 3 == 0 else 2
    tile = lax.switch(
        jnp.asarray(roles, jnp.int32)[spot.rank],
        [
            lambda item, square: item,
            lambda item, square: solve_square(item),
            solve_wide,
        ],
        tile,
        gram,
    )
    back = spot.give_back(tile, kinds)
    step_att, step_fc1, step_fc2 = [], [], []
    for layer in range(LAYERS):
        step_att.append(spot.att_back(back[3 * layer][:, : tp_count * att_cols]))
        step_fc1.append(back[3 * layer + 1][:, :ff_cols])
        step_fc2.append(back[3 * layer + 2][:, :ff_cols])
    step_att, step_fc1, step_fc2 = jnp.stack(step_att), jnp.stack(step_fc1), jnp.stack(step_fc2)
    keep_factor = 1.0 - muon_rate * muon_decay
    att_step = muon_rate * 0.2 * math.sqrt(D)
    mlp_step = muon_rate * 0.2 * math.sqrt(FF)

    def split_att(packed):
        query, key, value, out = jnp.split(packed, 4, axis=2)
        return query, key, value, flip(out)

    def stepped(weight, update, size):
        return weight * keep_factor - size * widened(update)

    update_query, update_key, update_value, update_out = split_att(step_att)
    new_query = stepped(w_query, update_query, att_step)
    new_key = stepped(w_key, update_key, att_step)
    new_value = stepped(w_value, update_value, att_step)
    new_out = stepped(w_out, update_out, att_step)
    new_fc1 = stepped(w_fc1, step_fc1, mlp_step)
    new_fc2 = stepped(w_fc2, flip(step_fc2), mlp_step)
    grad_query, grad_key, grad_value, grad_out = split_att(jnp.stack(sum_att))
    grad_fc1 = jnp.stack(sum_fc1)
    grad_fc2 = flip(jnp.stack(sum_fc2))
    moments = (mom_query, mom_key, mom_value, mom_out, mom_fc1, mom_fc2)
    grads = (grad_query, grad_key, grad_value, grad_out, grad_fc1, grad_fc2)
    new_moments = [muon_beta * moment + gradient for moment, gradient in zip(moments, grads)]
    new_vectors, new_vec_first, new_vec_second = adam(vectors, vec_first, vec_second, grad_vectors)
    new_fc1_bias, new_bias_first, new_bias_second = adam(
        fc1_bias, bias_first, bias_second, grad_fc1_bias
    )
    return (
        tokens_out,
        input_grad,
        grad_query,
        grad_key,
        grad_value,
        grad_out,
        grad_fc1,
        grad_fc2,
        grad_vectors,
        grad_fc1_bias,
        new_query,
        new_key,
        new_value,
        new_out,
        new_fc1,
        new_fc2,
        new_moments[0],
        new_moments[1],
        new_moments[2],
        new_moments[3],
        new_moments[4],
        new_moments[5],
        new_vectors,
        new_fc1_bias,
        new_vec_first,
        new_vec_second,
        new_bias_first,
        new_bias_second,
    )


def solution(mesh):
    placed = (
        P("fsdp", None, None),
        P("fsdp", None, None),
        P(None, "fsdp", "tp"),
        P(None, "fsdp", "tp"),
        P(None, "fsdp", "tp"),
        P(None, "tp", "fsdp"),
        P(None, "fsdp", "tp"),
        P(None, "tp", "fsdp"),
        P(None, "fsdp", "tp"),
        P(None, "fsdp", "tp"),
        P(None, "fsdp", "tp"),
        P(None, "tp", "fsdp"),
        P(None, "fsdp", "tp"),
        P(None, "tp", "fsdp"),
        P(),
        P(),
        P(),
        P(),
        P(),
        P(),
    )
    return jax.shard_map(
        per_device,
        mesh=mesh,
        in_specs=placed,
        out_specs=(
            P("fsdp", None, None),
            P("fsdp", None, None),
            P(None, "fsdp", "tp"),
            P(None, "fsdp", "tp"),
            P(None, "fsdp", "tp"),
            P(None, "tp", "fsdp"),
            P(None, "fsdp", "tp"),
            P(None, "tp", "fsdp"),
            P(),
            P(),
            P(None, "fsdp", "tp"),
            P(None, "fsdp", "tp"),
            P(None, "fsdp", "tp"),
            P(None, "tp", "fsdp"),
            P(None, "fsdp", "tp"),
            P(None, "tp", "fsdp"),
            P(None, "fsdp", "tp"),
            P(None, "fsdp", "tp"),
            P(None, "fsdp", "tp"),
            P(None, "tp", "fsdp"),
            P(None, "fsdp", "tp"),
            P(None, "tp", "fsdp"),
            P(),
            P(),
            P(),
            P(),
            P(),
            P(),
        ),
        check_vma=False,
    )
```
